512 devices in a mesh: section: 4 (over x), elem: 128 (over y, z, core).
Axes of the slice: x: 4, y: 8, z: 8, core: 2. Of those that a mesh axis runs over, the one named last changes fastest.
Arguments:
- interior_res: bfloat16 [3, 128, 4, 48, 100], P(None, 'elem', 'section'), may hold values from -1.5 to 1.5
- face_res: bfloat16 [3, 128, 4, 48, 4, 50], P(None, 'elem', 'section'), may hold values from -1.5 to 1.5
- trace_vals: bfloat16 [3, 128, 4, 48, 4, 50], P(None, 'elem', 'section'), may hold values from -1.5 to 1.5
- stabil: bfloat16 [128, 4, 48, 4, 25], P('elem'), may hold values from -2.5 to 2.5
- element_faces: int32 [128, 4, 48, 4], P('elem'), may hold values from 0 to 49151, as said below
- orient: int32 [128, 4, 48, 4, 10], P('elem'), may hold values from 0 to 9, as said below
- lift_matrix: bfloat16 [4, 20, 10], replicated, may hold values from -2 to 2
- face_matrix: bfloat16 [10, 10], replicated, may hold values from -2 to 2
- factors: bfloat16 [4, 128, 100, 19200], P('section', 'elem'), may hold values from -0.625 to 0.625
Outputs:
- trace_residual: float32 [3, 49152, 50], P(None, ('section', 'elem'))
- schur_product: float32 [3, 49152, 50], P(None, ('section', 'elem'))
The draws below stay inside these ranges and needn't reach their ends.
Inputs may be any that keep to these rules, and one draw needn't show every extreme that they name: `element_faces`: every face number is named by exactly two element faces. Face f is owned by column (f // 96) % 128. For every other column, exactly 2 of a column's element faces name faces owned by that column; the rest name faces owned by the column itself. `orient`: each row of 10 numbers is one of the six node orders that the symmetries of a triangle give to the ten nodes of its degree-3 lattice.
All inputs are finite; a program needn't handle non-finite values.
Results may differ from the reference program's by a relative error of at most 0.004.
Values may be sent and summed in bfloat16 or wider, within the bound.
No kernel may reach another device: no remote copies, remote signals or barrier semaphores. Data moves between devices by JAX's collectives and lax.ppermute only.
A program may use at most 128 MiB of HBM per device.

```python
import jax
import jax.numpy as jnp
import numpy as np
from jax import lax

VARS = 5
MODES = 20
FNODES = 10
ELEMS = 48
NI = 100
NF = 50
COLS = 128
COL_ELEMS = 192
GROUP_ELEMS = 64
SHARE = 2
FACE_DEV = 96
FACES = 49152
N_SECTION = 4


def triangle_table():
    lattice = [(first, second, 3 - first - second) for first in range(4) for second in range(4 - first)]
    rotations = [(0, 1, 2), (1, 2, 0), (2, 0, 1), (0, 2, 1), (2, 1, 0), (1, 0, 2)]
    table_rows = []
    for rotation in rotations:
        table_rows.append([lattice.index(tuple((point[corner] for corner in rotation))) for point in lattice])
    return np.array(table_rows, dtype=np.int32)


def draw_orient(key, part):
    symmetry = jax.random.randint(jax.random.fold_in(key, 5), (COLS, 4, ELEMS, 4), 0, 6)
    return jnp.asarray(triangle_table())[symmetry].astype(jnp.int32)


def draw_element_faces(key, part):
    item_count = 16 * ELEMS
    owned_count = 8 * ELEMS
    pair_faces = 2 * SHARE
    boundary_count = (COLS - 1) * pair_faces
    column_keys = jax.random.split(jax.random.fold_in(key, 11), COLS)
    owner_keys = jax.random.split(jax.random.fold_in(key, 12), COLS)
    orders = jax.vmap(lambda subkey: jax.random.permutation(subkey, item_count))(column_keys)
    places = jnp.argsort(orders, axis=1).astype(jnp.int32)
    columns = jnp.arange(COLS, dtype=jnp.int32)[:, None]
    boundary = places < boundary_count
    distance = places // pair_faces + 1
    within = places % pair_faces
    other_col = (columns + distance) % COLS
    self_owns = within < SHARE
    boundary_owner = jnp.where(self_owns, columns, other_col)
    boundary_number = jnp.where(self_owns, (distance - 1) * SHARE + within, (COLS - distance - 1) * SHARE + (within - SHARE))
    inner_number = (COLS - 1) * SHARE + (places - boundary_count) // 2
    owner = jnp.where(boundary, boundary_owner, columns)
    number = jnp.where(boundary, boundary_number, inner_number)
    owner_orders = jax.vmap(lambda subkey: jax.random.permutation(subkey, owned_count))(owner_keys)
    slot_place = owner_orders[owner, number]
    block = slot_place // FACE_DEV
    within_block = slot_place % FACE_DEV
    face = (block * COLS + owner) * FACE_DEV + within_block
    return face.reshape(COLS, 4, ELEMS, 4).astype(jnp.int32)


def level_of(own_key, extent, shards, least, high):
    gain, own = 1.0, jax.random.fold_in(own_key, 6)
    for position, shards_of in shards:
        heights = jnp.exp(jax.random.uniform(jax.random.fold_in(own, position), (shards_of,), jnp.float32, least / len(shards), high / len(shards)))
        gain = gain * jnp.repeat(heights, extent[position] // shards_of).reshape([-1 if axis == position else 1 for axis in range(len(extent))])
    return gain


def bell_draw(own_key, extent, deviation, bound, pieces=(), kind=jnp.bfloat16):
    drawn = deviation * jax.random.normal(own_key, extent, jnp.float32)
    if pieces:
        drawn = drawn * level_of(own_key, extent, pieces, -0.22, 0.18)
    return jnp.clip(drawn, -bound, bound).astype(kind)


def setup_inputs(seed: int = 0) -> dict:
    keys = jax.random.split(jax.random.key(seed), 10)
    interior_res = bell_draw(keys[0], (3, COLS, N_SECTION, ELEMS, NI), 0.25, 1.5, ((1, 128), (2, 4)))
    face_res = bell_draw(keys[1], (3, COLS, N_SECTION, ELEMS, 4, NF), 0.25, 1.5, ((1, 128), (2, 4)))
    trace_vals = bell_draw(keys[2], (3, COLS, N_SECTION, ELEMS, 4, NF), 0.25, 1.5, ((1, 128), (2, 4)))
    stabil = bell_draw(keys[3], (COLS, N_SECTION, ELEMS, 4, VARS * VARS), VARS ** -0.5, 2.5, ((0, 128),))
    element_faces = draw_element_faces(jax.random.fold_in(keys[9], 71), 0)
    orient = draw_orient(jax.random.fold_in(keys[9], 71), 0)
    lift_matrix = bell_draw(keys[6], (4, MODES, FNODES), FNODES ** -0.5, 2.0)
    face_matrix = bell_draw(keys[7], (FNODES, FNODES), FNODES ** -0.5, 2.0)
    factors = bell_draw(keys[8], (N_SECTION, COLS, NI, COL_ELEMS * NI), NI ** -0.5, 0.625, ((0, 4), (1, 128)))
    return {"interior_res": interior_res, "face_res": face_res, "trace_vals": trace_vals, "stabil": stabil, "element_faces": element_faces, "orient": orient, "lift_matrix": lift_matrix, "face_matrix": face_matrix, "factors": factors}


radau_inverse = ((4.3255798900631553510, 0.33919925181580986954, 0.54177053993587487119),
                 (-4.1787185915519047273, -0.32768282076106238708, 0.47662355450055045196),
                 (-0.50287263494578687595, 2.5719269498556054292, -0.59603920482822492497))


def transform(sections):
    values = sections.astype(jnp.float32)
    return jnp.stack([radau_inverse[row_index][0] * values[0] + radau_inverse[row_index][1] * values[1]
                      + radau_inverse[row_index][2] * values[2] for row_index in range(3)]).astype(jnp.bfloat16)


def reference(interior_res, face_res, trace_vals, stabil, element_faces, orient, lift_matrix, face_matrix, factors):
    highest = lax.Precision.HIGHEST
    lift_wide = lift_matrix.astype(jnp.float32)
    mass_wide = face_matrix.astype(jnp.float32)
    inner_all = jnp.moveaxis(transform(interior_res), 1, 0)
    face_all = jnp.moveaxis(transform(face_res), 1, 0)
    trace_all = jnp.moveaxis(transform(trace_vals), 1, 0)
    factor_all = jnp.moveaxis(factors, 1, 0)

    def alternate(block):
        return block.reshape(3, NI, 4, ELEMS // 3, NI).transpose(1, 2, 3, 0, 4).reshape(NI, COL_ELEMS, NI)

    def column_terms(packed_col):
        inner_w, face_w, trace_w, stabil_col, factor_col = packed_col
        inner_part = inner_w.reshape(3, COL_ELEMS, NI)
        face_part = face_w.reshape(3, COL_ELEMS, 4, FNODES, VARS).astype(jnp.float32)
        trace_part = trace_w.reshape(3, COL_ELEMS, 4, FNODES, VARS).astype(jnp.float32)
        stab_wide = stabil_col.reshape(COL_ELEMS, 4, VARS, VARS).astype(jnp.float32)
        weighted = jnp.einsum('ekvu,ceknu->ceknv', stab_wide, trace_part, precision=highest)
        lifted = jnp.einsum('kmn,ceknv->cemv', lift_wide, weighted, precision=highest)
        lifted = lifted.reshape(3, COL_ELEMS, NI).astype(jnp.bfloat16)
        right_sides = jnp.stack([inner_part, lifted], 1).astype(jnp.float32)
        real_inverse = factor_col[0].astype(jnp.float32).reshape(NI, COL_ELEMS, NI)
        first = jnp.einsum('iej,rej->rei', real_inverse, right_sides[0], precision=highest)
        real_part = alternate(factor_col[1:, :, :GROUP_ELEMS * NI].astype(jnp.float32))
        imag_part = alternate(factor_col[1:, :, GROUP_ELEMS * NI:2 * GROUP_ELEMS * NI].astype(jnp.float32))
        by_real = jnp.einsum('iej,crej->crei', real_part, right_sides[1:], precision=highest)
        by_imag = jnp.einsum('iej,crej->crei', imag_part, right_sides[1:], precision=highest)
        solved = jnp.stack([first, by_real[0] - by_imag[1], by_imag[0] + by_real[1]])
        shaped = solved.reshape(3, 2, COL_ELEMS, MODES, VARS)
        weighted_solve = jnp.einsum('ekvu,cremu->crekmv', stab_wide, shaped, precision=highest)
        coupled = jnp.einsum('kmn,crekmv->creknv', lift_wide, weighted_solve, precision=highest)
        face_term = jnp.einsum('nj,cekjv->ceknv', mass_wide, weighted, precision=highest)
        return jnp.stack([face_part - coupled[:, 0], face_term - coupled[:, 1]], 1)

    contribs = lax.map(column_terms, (inner_all, face_all, trace_all, stabil, factor_all))
    node_order = orient.reshape(COLS, 1, 1, COL_ELEMS, 4, FNODES, 1).astype(jnp.int32)
    oriented = jnp.take_along_axis(contribs, node_order, axis=5)
    item_rows = oriented.transpose(0, 3, 4, 1, 2, 5, 6).reshape(COLS * COL_ELEMS * 4, 6 * NF)
    summed = jax.ops.segment_sum(item_rows, element_faces.reshape(-1), num_segments=FACES)
    summed = summed.reshape(FACES, 3, 2, NF)
    return summed[:, :, 0].transpose(1, 0, 2), summed[:, :, 1].transpose(1, 0, 2)
```

```python
import jax
import jax.numpy as jnp
import numpy as np
from jax import lax
from jax.experimental import pallas as pl
from jax.experimental.pallas import tpu as pltpu
from jax.sharding import PartitionSpec as P

TI = (
    (4.325579890063155, 0.33919925181580984, 0.5417705399358749),
    (-4.178718591551905, -0.32768282076106237, 0.47662355450055044),
    (-0.5028726349457868, 2.571926949855605, -0.5960392048282249),
)
VARS, MODES, FN, NI, NF = 5, 20, 10, 100, 50
ELEMS, COLE, GRP, COLS, FDEV = 48, 192, 64, 128, 96
SLOTS = 4 * FDEV
W = 512
UW = VARS * W
CH = 3200
BF, F32, I32 = jnp.bfloat16, jnp.float32, jnp.int32
VMEM = pl.BlockSpec(memory_space=pltpu.VMEM)


def code_tables():
    cols = np.full((16, UW), -1, np.int32)
    for u in range(VARS):
        for k in range(4):
            for o in range(2):
                for n in range(FN):
                    for v in range(VARS):
                        lane = u * W + k * 128 + o * 64 + n * VARS + v
                        cols[0, lane] = k * 25 + v * 5 + u
                        cols[1, lane] = k * 5 + u
                        cols[2, lane] = o * FN + n
                        cols[3, lane] = k * FN + n
                        cols[4, lane] = u * 2 + o
                        cols[5, lane] = v if o == 0 else -1
                        cols[7, lane] = o
                        cols[8, lane] = k * NF + n * VARS + v if o == 0 else -1
    lanes = np.arange(UW) % 128
    cols[6] = np.where(cols[0] < 0, lanes, (lanes // 64) * 64 + (lanes % 64) % 5)
    rows = np.full((256, 128), -1, np.int32)
    for i in range(200):
        rows[i, 0] = (i // 50) * 5 + i % 5
        rows[i, 1] = (i % 50) // 5
    for x in range(2):
        for i in range(NI):
            rows[x * 128 + i, 2] = (i % 5) * 2 + x
            rows[x * 128 + i, 3] = i // 5
            rows[x * 128 + i, 4] = i % 5
    lane = np.arange(CH)
    tiles = np.zeros((8, CH), np.int32)
    tiles[0] = lane % NI
    tiles[1] = lane // NI
    return cols, rows, tiles


COL_CODES, ROW_CODES, TILE_CODES = code_tables()


def dot(a, b):
    return lax.dot_general(a, b, (((1,), (0,)), ((), ())), preferred_element_type=F32)


def dot_t(a, b):
    return lax.dot_general(a, b, (((1,), (1,)), ((), ())), preferred_element_type=F32)


def iota(shape, dim):
    return lax.broadcasted_iota(I32, shape, dim)


def onehot(cond):
    return jnp.where(cond, 1.0, 0.0).astype(BF)


def split(x):
    hi = x.astype(BF)
    return hi, (x - hi.astype(F32)).astype(BF)


def pack_kernel(inner_ref, face_ref, trace_ref, out_ref):
    out_ref[...] = jnp.zeros(out_ref.shape, BF)
    row = iota((ELEMS, ELEMS), 0)
    pick = onehot(iota((ELEMS, ELEMS), 1) == 3 * (row & 15) + (row >> 4))
    for ref, lane, width in ((inner_ref, 0, NI), (face_ref, 128, 4 * NF), (trace_ref, 384, 4 * NF)):
        vals = [ref[t].astype(F32) for t in range(3)]
        for g in range(3):
            mixed = (TI[g][0] * vals[0] + TI[g][1] * vals[1] + TI[g][2] * vals[2]).astype(BF)
            if g == 0:
                out_ref[0, :, lane : lane + width] = mixed
            else:
                moved = dot(pick, mixed).astype(BF)
                for t in range(3):
                    out_ref[1 + t, 16 * (g - 1) : 16 * g, lane : lane + width] = moved[
                        16 * t : 16 * t + 16
                    ]


def prep_kernel(
    where_ref, stab_ref, orient_ref, faces_ref, lift_ref, mass_ref, cols_ref, rows_ref, tiles_ref,
    s_ref, gg_ref, qq_ref, lm_ref, p0_ref, idx_ref, ab_ref, out_hot_ref, loc_hot_ref, tile_ref, bd_ref,
):
    section = where_ref[0]
    column = where_ref[1]
    row = iota((COLE, COLE), 0)
    third = section - 1
    target = jnp.where(
        section == 0, row, jnp.where(row < GRP, 48 * (row >> 4) + 3 * (row & 15) + third, -1)
    )
    pick = onehot(target == iota((COLE, COLE), 1))
    stab = dot(pick, stab_ref[...]).astype(BF)
    orient = dot(pick, orient_ref[...]).astype(BF)
    spread_kn = onehot(iota((40, UW), 0) == cols_ref[3:4, :])
    for u in range(VARS):
        cut = slice(u * W, (u + 1) * W)
        expand = onehot(iota((100, W), 0) == cols_ref[0:1, cut])
        s_ref[:, cut] = dot(stab, expand)
    nodes = dot(orient, spread_kn[:, :W])
    idx_ref[...] = (VARS * nodes).astype(I32) + cols_ref[6:7, :W]
    pick_j = onehot(rows_ref[:, 1:2] == iota((256, FN), 1))
    mass = dot_t(pick_j, mass_ref[...]).astype(BF)
    pick_m = onehot(rows_ref[:, 3:4] == iota((256, MODES), 1))
    lift = dot(pick_m, lift_ref[...]).astype(BF)
    for u in range(VARS):
        cut = slice(u * W, (u + 1) * W)
        plain = onehot(iota((FN, W), 0) == cols_ref[2:3, cut])
        massed = onehot(iota((FN, W), 0) + FN == cols_ref[2:3, cut])
        full = dot(pick_j, plain) + dot(mass, massed)
        gg_ref[:, cut] = jnp.where(rows_ref[:, 0:1] == cols_ref[1:2, cut], full, 0.0).astype(BF)
        full = dot(lift, spread_kn[:, cut])
        qq_ref[:, cut] = jnp.where(rows_ref[:, 2:3] == cols_ref[4:5, cut], full, 0.0).astype(BF)
        if u == 0:
            keep = rows_ref[:128, 4:5] == cols_ref[5:6, cut]
            keep = keep & (cols_ref[5:6, cut] >= 0)
            lm_ref[...] = jnp.where(keep, full[:128], 0.0).astype(BF)
    p0_ref[...] = onehot(iota((256, W), 0) == cols_ref[8:9, :W])
    tile_ref[...] = onehot(iota((128, CH), 0) == tiles_ref[0:1, :])
    bd_ref[...] = jnp.where(iota((32, CH), 0) == tiles_ref[1:2, :], 1.0, 0.0)
    face = faces_ref[...]
    block = ((face >> 5) * 43691) >> 17
    owner = block & (COLS - 1)
    slot = (block >> 7) * FDEV + face - block * FDEV
    away = owner != column
    lane = iota((COLE, 16), 1)
    codes = jnp.zeros((COLE, 16), I32)
    fields = (jnp.where(away, owner + 1, 0), jnp.where(away, 0, 1), slot >> 5, slot & 31)
    for f, field in enumerate(fields):
        for k in range(4):
            codes = jnp.where(lane == 4 * f + k, field[:, k : k + 1], codes)
    codes = dot(pick, codes.astype(F32).astype(BF))
    ab_ref[...] = codes
    turned = dot_t(onehot(iota((16, 16), 0) == iota((16, 16), 1)), codes.astype(BF))
    before = onehot(iota((COLE, COLE), 0) < iota((COLE, COLE), 1))
    count = jnp.zeros((COLS, 1), F32)
    own_iota = iota((COLS, COLE), 0) + 1
    for k in range(4):
        own = turned[k : k + 1, :].astype(I32)
        hot = own_iota == own
        hot_f = jnp.where(hot, 1.0, 0.0)
        rank = dot(hot_f.astype(BF), before) + count
        count = count + jnp.sum(hot_f, axis=1, keepdims=True)
        rank = jnp.sum(jnp.where(hot, rank, 0.0), axis=0, keepdims=True).astype(I32)
        key = jnp.where(own > 0, 2 * (own - 1) + rank, -1)
        out_hot_ref[k] = onehot(iota((2 * COLS, COLE), 0) == key)
        slots = (32.0 * turned[8 + k : 9 + k, :] + turned[12 + k : 13 + k, :]).astype(I32)
        slots = jnp.where(turned[4 + k : 5 + k, :] > 0.5, slots, -1)
        loc_hot_ref[k] = onehot(iota((SLOTS, COLE), 0) == slots)


def main_kernel(
    where_ref, rec_ref, s_ref, gg_ref, qq_ref, lm_ref, p0_ref, idx_ref, ab_ref, hot_ref, tile_ref,
    bd_ref, cols_ref, factor_ref, pay_ref, con_ref, fac_ref, sol_ref, sem_ref,
):
    section = where_ref[0]

    def fetch(c):
        cut = pl.ds(c * CH, CH)
        return pltpu.make_async_copy(factor_ref.at[:, cut], fac_ref.at[:, cut], sem_ref.at[c])

    def finish(x_in, number, parts, solve):
        total = number * parts

        def s_of(u):
            s = s_ref[:number, u * W : (u + 1) * W]
            return jnp.concatenate([s] * parts, axis=0) if parts > 1 else s

        trace = x_in[:, 384:640]
        value = jnp.zeros((total, W), F32)
        for u in range(VARS):
            value = value + s_of(u) * dot(trace, gg_ref[:, u * W : (u + 1) * W])
        hi, lo = split(value)
        lifted = (dot_t(hi, lm_ref[...]) + dot_t(lo, lm_ref[...])).astype(BF)
        sol_ref[...] = jnp.zeros(sol_ref.shape, F32)
        solve(x_in[:, :128], lifted)
        hi, lo = split(sol_ref[:total, :])
        base = jnp.where(cols_ref[7:8, :W] == 1, value, 0.0) + dot(x_in[:, 128:384], p0_ref[...])
        for u in range(VARS):
            cut = slice(u * W, (u + 1) * W)
            base = base - s_of(u) * (dot(hi, qq_ref[:, cut]) + dot(lo, qq_ref[:, cut]))
        con_ref[...] = jnp.zeros(con_ref.shape, BF)
        lane = iota((number, 128), 1)
        pay = [jnp.zeros((2 * COLS, 128), F32) for _ in range(parts)]
        for k in range(4):
            index = idx_ref[:number, 128 * k : 128 * k + 128]
            for c in range(parts):
                piece = base[c * number : (c + 1) * number, 128 * k : 128 * k + 128]
                piece = jnp.take_along_axis(piece, index, axis=1, mode="promise_in_bounds")
                if c == 0:
                    piece = jnp.where(lane == NF, ab_ref[:number, 8 + k : 9 + k], piece)
                    piece = jnp.where(lane == NF + 1, ab_ref[:number, 12 + k : 13 + k], piece)
                piece = piece.astype(BF)
                con_ref[k, :number, 128 * c : 128 * c + 128] = piece
                pay[c] = pay[c] + dot(hot_ref[k, :, :number], piece)
        for c in range(2):
            pay_ref[:, 128 * c : 128 * c + 128] = (
                pay[c].astype(BF) if c < parts else jnp.zeros((2 * COLS, 128), BF)
            )

    @pl.when(section == 0)
    def _():
        for c in range(6):
            fetch(c).start()
        x_in = jnp.concatenate([rec_ref[s] for s in range(4)], axis=0)

        def solve(inner, lifted):
            keep = jnp.concatenate([bd_ref[...]] * 2, axis=0)
            for c in range(6):
                cut = slice(32 * c, 32 * c + 32)
                x = jnp.concatenate([inner[cut], lifted[cut]], axis=0)
                x = (dot(x, tile_ref[...]) * keep).astype(BF)
                fetch(c).wait()
                y = dot_t(x, fac_ref[:, c * CH : (c + 1) * CH])
                sol_ref[cut, 0:NI] = y[:32]
                sol_ref[cut, 128 : 128 + NI] = y[32:]

        finish(x_in, COLE, 1, solve)

    @pl.when(section != 0)
    def _():
        for c in range(4):
            fetch(c).start()
        x_in = jnp.concatenate(
            [rec_ref[s, 16 * g : 16 * g + 16] for g in range(2) for s in range(4)], axis=0
        )

        def solve(inner, lifted):
            keep = jnp.concatenate([bd_ref[...]] * 4, axis=0)
            waited = []
            for c in range(2):
                re = slice(32 * c, 32 * c + 32)
                im = slice(GRP + 32 * c, GRP + 32 * c + 32)
                x = jnp.concatenate([inner[re], lifted[re], inner[im], lifted[im]], axis=0)
                x = (dot(x, tile_ref[...]) * keep).astype(BF)
                fetch(c).wait()
                a = dot_t(x, fac_ref[:, c * CH : (c + 1) * CH])
                fetch(2 + c).wait()
                b = dot_t(x, fac_ref[:, (2 + c) * CH : (3 + c) * CH])
                real = a[:64] - b[64:]
                imag = b[:64] + a[64:]
                sol_ref[re, 0:NI] = real[:32]
                sol_ref[re, 128 : 128 + NI] = real[32:]
                sol_ref[im, 0:NI] = imag[:32]
                sol_ref[im, 128 : 128 + NI] = imag[32:]

        finish(x_in, GRP, 2, solve)


def local_kernel(hot_ref, con_ref, out_ref):
    total = dot(hot_ref[0], con_ref[0])
    for k in range(1, 4):
        total = total + dot(hot_ref[k], con_ref[k])
    out_ref[...] = total


def place_kernel(got_ref, loc_ref, out_ref):
    got = got_ref[...]
    lane = iota((8, 128), 1)
    weights = jnp.where(lane == NF, 32.0, jnp.where(lane == NF + 1, 1.0, 0.0)).astype(BF)
    slot = dot_t(weights, got[:, :128])[0:1].astype(I32)
    hot = onehot(iota((SLOTS, 2 * COLS), 0) == slot)
    total = loc_ref[...] + dot(hot, got)
    for s in range(4):
        out_ref[s] = total[FDEV * s : FDEV * s + FDEV].astype(BF)


def sum_kernel(got_ref, res_ref, schur_ref):
    sums = [
        got_ref[0, :, :128].astype(F32),
        got_ref[1, :, :128].astype(F32)
        + got_ref[2, :, :128].astype(F32)
        + got_ref[3, :, :128].astype(F32),
        got_ref[1, :, 128:].astype(F32)
        + got_ref[2, :, 128:].astype(F32)
        + got_ref[3, :, 128:].astype(F32),
    ]
    for g in range(3):
        res_ref[g] = sums[g][:, :NF]
        schur_ref[g] = pltpu.roll(sums[g], 64, 1)[:, :NF]


def shape(dims, kind):
    return jax.ShapeDtypeStruct(dims, kind)


def cost(flops, nbytes):
    return pl.CostEstimate(flops=flops, bytes_accessed=nbytes, transcendentals=0)


def on_device(
    interior_res, face_res, trace_vals, stabil, element_faces, orient, lift_matrix, face_matrix, factors
):
    smem = pl.BlockSpec(memory_space=pltpu.SMEM)
    where = jnp.stack([lax.axis_index("section"), lax.axis_index("elem")]).astype(I32)
    params = pltpu.CompilerParams(vmem_limit_bytes=56 * 2**20)
    send = pl.pallas_call(
        pack_kernel,
        name="pack",
        out_shape=shape((4, ELEMS, 640), BF),
        in_specs=[VMEM] * 3,
        out_specs=VMEM,
        cost_estimate=cost(10**8, 10**6),
    )(
        interior_res.reshape(3, ELEMS, NI),
        face_res.reshape(3, ELEMS, 4 * NF),
        trace_vals.reshape(3, ELEMS, 4 * NF),
    )
    received = lax.all_to_all(send, "section", split_axis=0, concat_axis=0, tiled=True)
    cols, rows, tiles = jnp.asarray(COL_CODES), jnp.asarray(ROW_CODES), jnp.asarray(TILE_CODES)
    s_all, gg, qq, lm, p0, idx, ab, out_hot, loc_hot, tile, bd = pl.pallas_call(
        prep_kernel,
        name="prep",
        out_shape=(
            shape((COLE, UW), F32),
            shape((256, UW), BF),
            shape((256, UW), BF),
            shape((128, W), BF),
            shape((256, W), BF),
            shape((COLE, W), I32),
            shape((COLE, 16), F32),
            shape((4, 2 * COLS, COLE), BF),
            shape((4, SLOTS, COLE), BF),
            shape((128, CH), BF),
            shape((32, CH), F32),
        ),
        in_specs=[smem] + [VMEM] * 8,
        out_specs=[VMEM] * 11,
        compiler_params=params,
        cost_estimate=cost(10**9, 8 * 10**6),
    )(
        where,
        stabil.reshape(COLE, 100),
        orient.reshape(COLE, 40).astype(BF),
        element_faces.reshape(COLE, 4),
        lift_matrix.transpose(1, 0, 2).reshape(MODES, 4 * FN),
        face_matrix,
        cols,
        rows,
        tiles,
    )
    payload, contrib = pl.pallas_call(
        main_kernel,
        name="condense",
        out_shape=(shape((2 * COLS, 256), BF), shape((4, COLE, 256), BF)),
        in_specs=[smem] + [VMEM] * 12 + [pl.BlockSpec(memory_space=pl.ANY)],
        out_specs=[VMEM] * 2,
        scratch_shapes=[
            pltpu.VMEM((NI, COLE * NI), BF),
            pltpu.VMEM((COLE, 256), F32),
            pltpu.SemaphoreType.DMA((6,)),
        ],
        compiler_params=params,
        cost_estimate=cost(10**9, 8 * 10**6),
    )(
        where, received, s_all, gg, qq, lm, p0, idx, ab, out_hot, tile, bd, cols,
        factors.reshape(NI, COLE * NI),
    )
    got = lax.all_to_all(
        payload.reshape(COLS, 2, 256), "elem", split_axis=0, concat_axis=0, tiled=True
    )
    local = pl.pallas_call(
        local_kernel,
        name="local",
        out_shape=shape((SLOTS, 256), F32),
        in_specs=[VMEM] * 2,
        out_specs=VMEM,
        cost_estimate=cost(3 * 10**8, 2 * 10**6),
    )(loc_hot, contrib)
    partial = pl.pallas_call(
        place_kernel,
        name="place",
        out_shape=shape((4, FDEV, 256), BF),
        in_specs=[VMEM] * 2,
        out_specs=VMEM,
        cost_estimate=cost(10**8, 10**6),
    )(got.reshape(2 * COLS, 256), local)
    parts = lax.all_to_all(partial, "section", split_axis=0, concat_axis=0, tiled=True)
    return tuple(
        pl.pallas_call(
            sum_kernel,
            name="total",
            out_shape=(shape((3, FDEV, NF), F32), shape((3, FDEV, NF), F32)),
            in_specs=[VMEM],
            out_specs=[VMEM] * 2,
            cost_estimate=cost(10**6, 10**6),
        )(parts)
    )


def solution(mesh):
    return jax.shard_map(
        on_device,
        mesh=mesh,
        in_specs=(
            P(None, "elem", "section", None, None),
            P(None, "elem", "section", None, None, None),
            P(None, "elem", "section", None, None, None),
            P("elem", None, None, None, None),
            P("elem", None, None, None),
            P("elem", None, None, None, None),
            P(),
            P(),
            P("section", "elem", None, None),
        ),
        out_specs=(P(None, ("section", "elem"), None), P(None, ("section", "elem"), None)),
        check_vma=False,
    )
```

```python
import jax
import jax.numpy as jnp
import numpy as np
from jax import lax
from jax.experimental import pallas as pl
from jax.experimental.pallas import tpu as pltpu
from jax.sharding import PartitionSpec as P

TI = (
    (4.325579890063155, 0.33919925181580984, 0.5417705399358749),
    (-4.178718591551905, -0.32768282076106237, 0.47662355450055044),
    (-0.5028726349457868, 2.571926949855605, -0.5960392048282249),
)
VARS, MODES, FN, NI, NF = 5, 20, 10, 100, 50
ELEMS, COLE, GRP, COLS, FDEV = 48, 192, 64, 128, 96
SLOTS = 4 * FDEV
W = 512
UW = VARS * W
CH = 3200
BF, F32, I32 = jnp.bfloat16, jnp.float32, jnp.int32
VMEM = pl.BlockSpec(memory_space=pltpu.VMEM)


def code_tables():
    cols = np.full((16, UW), -1, np.int32)
    for u in range(VARS):
        for k in range(4):
            for o in range(2):
                for n in range(FN):
                    for v in range(VARS):
                        lane = u * W + k * 128 + o * 64 + n * VARS + v
                        cols[0, lane] = (v * 5 + u) * 4 + k
                        cols[1, lane] = k * 5 + u
                        cols[2, lane] = o * FN + n
                        cols[3, lane] = n * 4 + k
                        cols[4, lane] = u * 2 + o
                        cols[5, lane] = v if o == 0 else -1
                        cols[7, lane] = o
                        cols[8, lane] = k * 64 + n * VARS + v if o == 0 else -1
    lanes = np.arange(UW) % 128
    cols[6] = np.where(cols[0] < 0, lanes, (lanes // 64) * 64 + (lanes % 64) % 5)
    rows = np.full((256, 128), -1, np.int32)
    for i in range(256):
        if i % 64 < NF:
            rows[i, 0] = (i // 64) * 5 + i % 64 % 5
            rows[i, 1] = i % 64 // 5
    for x in range(2):
        for i in range(NI):
            rows[x * 128 + i, 2] = (i % 5) * 2 + x
            rows[x * 128 + i, 3] = i // 5
            rows[x * 128 + i, 4] = i % 5
    lane = np.arange(CH)
    tiles = np.zeros((8, CH), np.int32)
    tiles[0] = lane % NI
    tiles[1] = lane // NI
    spread = (np.arange(128)[:, None] == lane[None, :] % NI).astype(np.float32)
    return cols, rows, tiles, spread


COL_CODES, ROW_CODES, TILE_CODES, TILE_SPREAD = code_tables()


def dot(a, b):
    return lax.dot_general(a, b, (((1,), (0,)), ((), ())), preferred_element_type=F32)


def dot_t(a, b):
    return lax.dot_general(a, b, (((1,), (1,)), ((), ())), preferred_element_type=F32)


def iota(shape, dim):
    return lax.broadcasted_iota(I32, shape, dim)


def onehot(cond):
    return jnp.where(cond, 1.0, 0.0).astype(BF)


def split(x):
    hi = x.astype(BF)
    return hi, (x - hi.astype(F32)).astype(BF)


def pack_kernel(inner_ref, face_ref, trace_ref, out_ref, mix_ref):
    out_ref[...] = jnp.zeros(out_ref.shape, BF)
    mix_ref[...] = jnp.zeros(mix_ref.shape, BF)

    def place(g, lane, piece):
        cut = slice(lane, lane + piece.shape[1])
        if g == 0:
            out_ref[0, :, cut] = piece
        else:
            mix_ref[g - 1, :, cut] = piece

    for ref, lane in ((inner_ref, 0), (face_ref, 128), (trace_ref, 384)):
        vals = [ref[t].astype(F32) for t in range(3)]
        for g in range(3):
            mixed = TI[g][0] * vals[0] + TI[g][1] * vals[1] + TI[g][2] * vals[2]
            if lane == 0:
                place(g, 0, mixed.astype(BF))
            else:
                for k in range(4):
                    place(g, lane + 64 * k, mixed[:, k, :].astype(BF))
    row = iota((ELEMS, ELEMS), 0)
    pick = onehot(iota((ELEMS, ELEMS), 1) == 3 * (row & 15) + (row >> 4))
    for g in range(2):
        moved = dot(pick, mix_ref[g]).astype(BF)
        for t in range(3):
            out_ref[1 + t, 16 * g : 16 * g + 16, :] = moved[16 * t : 16 * t + 16]


def prep_kernel(
    stab_ref, orient_ref, faces_ref, lift_ref, mass_ref, cols_ref, rows_ref,
    s_ref, gg_ref, qq_ref, lm_ref, p0_ref, idx_ref, ab_ref, turned_ref, out_hot_ref,
):
    section = lax.axis_index("section")
    column = lax.axis_index("elem")
    row = iota((COLE, ELEMS), 0)
    third = section - 1
    target = jnp.where(
        section == 0, row, jnp.where(row < GRP, 48 * (row >> 4) + 3 * (row & 15) + third, -1)
    )
    face = faces_ref[...]
    block = ((face >> 5) * 43691) >> 17
    owner = block & (COLS - 1)
    slot = (block >> 7) * FDEV + face - block * FDEV
    away = owner != column
    fields = [jnp.where(away, owner + 1, 0), jnp.where(away, 0, 1), slot >> 5, slot & 31]
    fields = [field.astype(F32) for field in fields]
    stab = jnp.zeros((COLE, 100), F32)
    orient = jnp.zeros((COLE, 40), F32)
    codes = jnp.zeros((COLE, 16), F32)
    turned = jnp.zeros((16, COLE), F32)
    for s in range(4):
        pick = onehot(target == iota((COLE, ELEMS), 1) + ELEMS * s)
        stab = stab + dot_t(pick, stab_ref[s].astype(F32).reshape(100, ELEMS).astype(BF))
        orient = orient + dot_t(pick, orient_ref[s].astype(F32).reshape(40, ELEMS).astype(BF))
        field = jnp.concatenate([f[s] for f in fields], axis=0).astype(BF)
        codes = codes + dot_t(pick, field)
        turned = turned + dot_t(field, pick)
    ab_ref[...] = codes
    turned_ref[...] = turned
    stab = stab.astype(BF)
    spread_kn = onehot(iota((40, UW), 0) == cols_ref[3:4, :])
    for u in range(VARS):
        cut = slice(u * W, (u + 1) * W)
        expand = onehot(iota((100, W), 0) == cols_ref[0:1, cut])
        s_ref[:, cut] = dot(stab, expand).astype(BF)
    nodes = dot(orient.astype(BF), spread_kn[:, :W])
    idx_ref[...] = (VARS * nodes).astype(I32) + cols_ref[6:7, :W]
    pick_j = onehot(rows_ref[:, 1:2] == iota((256, FN), 1))
    eye = jnp.where(iota((FN, FN), 0) == iota((FN, FN), 1), 1.0, 0.0)
    mass = jnp.concatenate([eye, mass_ref[...].astype(F32)], axis=0).astype(BF)
    mass = dot_t(pick_j, mass).astype(BF)
    pick_m = onehot(rows_ref[:, 3:4] == iota((256, MODES), 1))
    lift = jnp.concatenate([lift_ref[n].astype(F32) for n in range(FN)], axis=0).astype(BF)
    lift = dot_t(pick_m, lift).astype(BF)
    for u in range(VARS):
        cut = slice(u * W, (u + 1) * W)
        full = dot(mass, onehot(iota((2 * FN, W), 0) == cols_ref[2:3, cut]))
        gg_ref[:, cut] = jnp.where(rows_ref[:, 0:1] == cols_ref[1:2, cut], full, 0.0).astype(BF)
        full = dot(lift, spread_kn[:, cut])
        qq_ref[:, cut] = jnp.where(rows_ref[:, 2:3] == cols_ref[4:5, cut], full, 0.0).astype(BF)
        if u == 0:
            keep = rows_ref[:128, 4:5] == cols_ref[5:6, cut]
            keep = keep & (cols_ref[5:6, cut] >= 0)
            lm_ref[...] = jnp.where(keep, full[:128], 0.0).astype(BF)
    p0_ref[...] = onehot(iota((256, W), 0) == cols_ref[8:9, :W])
    before = onehot(iota((COLE, COLE), 0) < iota((COLE, COLE), 1))
    count = jnp.zeros((COLS, 1), F32)
    own_iota = iota((COLS, COLE), 0) + 1
    for k in range(4):
        own = turned[k : k + 1, :].astype(I32)
        hot = own_iota == own
        hot_f = jnp.where(hot, 1.0, 0.0)
        rank = dot(hot_f.astype(BF), before) + count
        count = count + jnp.sum(hot_f, axis=1, keepdims=True)
        rank = jnp.sum(jnp.where(hot, rank, 0.0), axis=0, keepdims=True).astype(I32)
        key = jnp.where(own > 0, 2 * (own - 1) + rank, -1)
        out_hot_ref[k] = onehot(iota((2 * COLS, COLE), 0) == key)


def main_kernel(
    rec_ref, ab_ref, tiles_ref, cols_ref,
    s_hbm, gg_hbm, lm_hbm, tile_hbm, qq_hbm, p0_hbm, idx_hbm, hot_hbm, factor_ref,
    pay_ref, con_ref,
    s_ref, gg_ref, lm_ref, tile_ref, qq_ref, p0_ref, idx_ref, hot_ref, fac_ref, sol_ref, bd_ref,
    sem_ref, load_ref,
):
    section = lax.axis_index("section")
    pairs = (
        (gg_hbm, gg_ref), (s_hbm, s_ref), (lm_hbm, lm_ref), (tile_hbm, tile_ref), (qq_hbm, qq_ref),
        (p0_hbm, p0_ref), (idx_hbm, idx_ref), (hot_hbm, hot_ref),
    )

    def load(i):
        return pltpu.make_async_copy(pairs[i][0], pairs[i][1], load_ref.at[i])

    for i in range(4):
        load(i).start()

    def spread(x):
        total = x.shape[0]
        for j in range(5):
            cut = slice(640 * j, 640 * j + 640)
            keep = (iota((total, 640), 0) & 31) == tiles_ref[1:2, cut]
            bd_ref[:total, cut] = jnp.where(keep, dot(x, tile_ref[:, cut]), 0.0).astype(BF)

    def fetch(c):
        cut = pl.ds(c * CH, CH)
        return pltpu.make_async_copy(factor_ref.at[:, cut], fac_ref.at[:, cut], sem_ref.at[c])

    def finish(x_in, number, parts, solve):
        total = number * parts

        def s_of(u):
            s = s_ref[:number, u * W : (u + 1) * W].astype(F32)
            return jnp.concatenate([s] * parts, axis=0) if parts > 1 else s

        trace = x_in[:, 384:640]
        value = jnp.zeros((total, W), F32)
        load(0).wait()
        load(1).wait()
        for u in range(VARS):
            value = value + s_of(u) * dot(trace, gg_ref[:, u * W : (u + 1) * W])
        hi, lo = split(value)
        load(2).wait()
        lifted = (dot_t(hi, lm_ref[...]) + dot_t(lo, lm_ref[...])).astype(BF)
        sol_ref[...] = jnp.zeros(sol_ref.shape, F32)
        load(3).wait()
        solve(x_in[:, :128], lifted)
        hi, lo = split(sol_ref[:total, :])
        for i in range(4, 8):
            load(i).wait()
        base = jnp.where(cols_ref[7:8, :W] == 1, value, 0.0) + dot(x_in[:, 128:384], p0_ref[...])
        for u in range(VARS):
            cut = slice(u * W, (u + 1) * W)
            base = base - s_of(u) * (dot(hi, qq_ref[:, cut]) + dot(lo, qq_ref[:, cut]))
        con_ref[...] = jnp.zeros(con_ref.shape, BF)
        lane = iota((number, 128), 1)
        pay = [jnp.zeros((2 * COLS, 128), F32) for _ in range(parts)]
        for k in range(4):
            index = idx_ref[:number, 128 * k : 128 * k + 128]
            for c in range(parts):
                piece = base[c * number : (c + 1) * number, 128 * k : 128 * k + 128]
                piece = jnp.take_along_axis(piece, index, axis=1, mode="promise_in_bounds")
                if c == 0:
                    piece = jnp.where(lane == NF, ab_ref[:number, 8 + k : 9 + k], piece)
                    piece = jnp.where(lane == NF + 1, ab_ref[:number, 12 + k : 13 + k], piece)
                piece = piece.astype(BF)
                con_ref[k, :number, 128 * c : 128 * c + 128] = piece
                pay[c] = pay[c] + dot(hot_ref[k, :, :number], piece)
        if parts == 1:
            pay = pay + [jnp.zeros((2 * COLS, 128), F32)]
        pay = jnp.concatenate(pay, axis=1)
        pay_ref[...] = pay.reshape(COLS, 2, 256).astype(BF)

    @pl.when(section == 0)
    def _():
        for c in range(6):
            fetch(c).start()
        for i in range(4, 8):
            load(i).start()
        x_in = jnp.concatenate([rec_ref[s] for s in range(4)], axis=0)

        def solve(inner, lifted):
            cuts = [slice(32 * c, 32 * c + 32) for c in range(6)]
            spread(jnp.concatenate([a[cut] for cut in cuts for a in (inner, lifted)], axis=0))
            for c, cut in enumerate(cuts):
                fetch(c).wait()
                y = dot_t(bd_ref[64 * c : 64 * c + 64, :], fac_ref[:, c * CH : (c + 1) * CH])
                sol_ref[cut, 0:NI] = y[:32]
                sol_ref[cut, 128 : 128 + NI] = y[32:]

        finish(x_in, COLE, 1, solve)

    @pl.when(section != 0)
    def _():
        for c in range(4):
            fetch(c).start()
        for i in range(4, 8):
            load(i).start()
        x_in = jnp.concatenate(
            [rec_ref[s, 16 * g : 16 * g + 16] for g in range(2) for s in range(4)], axis=0
        )

        def solve(inner, lifted):
            res = [slice(32 * c, 32 * c + 32) for c in range(2)]
            ims = [slice(GRP + 32 * c, GRP + 32 * c + 32) for c in range(2)]
            spread(
                jnp.concatenate(
                    [a[cut] for c in range(2) for cut in (res[c], ims[c]) for a in (inner, lifted)],
                    axis=0,
                )
            )
            for c, (re, im) in enumerate(zip(res, ims)):
                x = bd_ref[128 * c : 128 * c + 128, :]
                fetch(c).wait()
                a = dot_t(x, fac_ref[:, c * CH : (c + 1) * CH])
                fetch(2 + c).wait()
                b = dot_t(x, fac_ref[:, (2 + c) * CH : (3 + c) * CH])
                real = a[:64] - b[64:]
                imag = b[:64] + a[64:]
                sol_ref[re, 0:NI] = real[:32]
                sol_ref[re, 128 : 128 + NI] = real[32:]
                sol_ref[im, 0:NI] = imag[:32]
                sol_ref[im, 128 : 128 + NI] = imag[32:]

        finish(x_in, GRP, 2, solve)


def local_kernel(turned_ref, con_ref, out_ref):
    total = jnp.zeros(out_ref.shape, F32)
    for k in range(4):
        slots = 32.0 * turned_ref[8 + k : 9 + k, :] + turned_ref[12 + k : 13 + k, :]
        slots = jnp.where(turned_ref[4 + k : 5 + k, :] > 0.5, slots, -1.0).astype(I32)
        total = total + dot(onehot(iota((SLOTS, COLE), 0) == slots), con_ref[k])
    out_ref[...] = total


def place_kernel(got_ref, loc_ref, out_ref):
    got = got_ref[...].astype(F32).reshape(2 * COLS, 256).astype(BF)
    lane = iota((8, 128), 1)
    weights = jnp.where(lane == NF, 32.0, jnp.where(lane == NF + 1, 1.0, 0.0)).astype(BF)
    slot = dot_t(weights, got[:, :128])[0:1].astype(I32)
    hot = onehot(iota((SLOTS, 2 * COLS), 0) == slot)
    total = loc_ref[...] + dot(hot, got)
    for s in range(4):
        out_ref[s] = total[FDEV * s : FDEV * s + FDEV].astype(BF)


def sum_kernel(got_ref, res_ref, schur_ref):
    three = got_ref[1].astype(F32) + got_ref[2].astype(F32) + got_ref[3].astype(F32)
    for g, part in enumerate((got_ref[0, :, :128].astype(F32), three[:, :128], three[:, 128:])):
        part = part.T
        res_ref[g] = part[:NF]
        schur_ref[g] = part[64 : 64 + NF]


def shape(dims, kind):
    return jax.ShapeDtypeStruct(dims, kind)


def hold(x):
    return pltpu.with_memory_space_constraint(x, pltpu.VMEM)


def cost(flops, nbytes):
    return pl.CostEstimate(flops=flops, bytes_accessed=nbytes, transcendentals=0)


def on_device(
    interior_res, face_res, trace_vals, stabil, element_faces, orient, lift_matrix, face_matrix, factors
):
    params = pltpu.CompilerParams(vmem_limit_bytes=59 * 2**20)
    send = pl.pallas_call(
        pack_kernel,
        name="pack",
        out_shape=shape((4, ELEMS, 640), BF),
        in_specs=[VMEM] * 3,
        out_specs=VMEM,
        scratch_shapes=[pltpu.VMEM((2, ELEMS, 640), BF)],
        compiler_params=params,
        cost_estimate=cost(10**8, 10**6),
    )(
        interior_res.reshape(3, ELEMS, NI),
        face_res.reshape(3, ELEMS, 4, NF),
        trace_vals.reshape(3, ELEMS, 4, NF),
    )
    received = hold(lax.all_to_all(send, "section", split_axis=0, concat_axis=0, tiled=True))
    cols, rows, tiles = jnp.asarray(COL_CODES), jnp.asarray(ROW_CODES), jnp.asarray(TILE_CODES)
    s_all, gg, qq, lm, p0, idx, ab, turned, out_hot = pl.pallas_call(
        prep_kernel,
        name="prep",
        out_shape=(
            shape((COLE, UW), BF),
            shape((256, UW), BF),
            shape((256, UW), BF),
            shape((128, W), BF),
            shape((256, W), BF),
            shape((COLE, W), I32),
            shape((COLE, 16), F32),
            shape((16, COLE), F32),
            shape((4, 2 * COLS, COLE), BF),
        ),
        in_specs=[VMEM] * 7,
        out_specs=[VMEM] * 9,
        compiler_params=params,
        cost_estimate=cost(10**9, 8 * 10**6),
    )(
        stabil[0].transpose(0, 3, 2, 1),
        orient[0].transpose(0, 3, 2, 1),
        element_faces[0].transpose(0, 2, 1),
        lift_matrix.transpose(2, 0, 1),
        face_matrix,
        cols,
        rows,
    )
    payload, contrib = pl.pallas_call(
        main_kernel,
        name="condense",
        out_shape=(shape((COLS, 2, 256), BF), shape((4, COLE, 256), BF)),
        in_specs=[VMEM] * 4 + [pl.BlockSpec(memory_space=pltpu.HBM)] * 9,
        out_specs=[VMEM] * 2,
        scratch_shapes=[
            pltpu.VMEM((COLE, UW), BF),
            pltpu.VMEM((256, UW), BF),
            pltpu.VMEM((128, W), BF),
            pltpu.VMEM((128, CH), BF),
            pltpu.VMEM((256, UW), BF),
            pltpu.VMEM((256, W), BF),
            pltpu.VMEM((COLE, W), I32),
            pltpu.VMEM((4, 2 * COLS, COLE), BF),
            pltpu.VMEM((NI, COLE * NI), BF),
            pltpu.VMEM((COLE, 256), F32),
            pltpu.VMEM((2 * COLE, CH), BF),
            pltpu.SemaphoreType.DMA((6,)),
            pltpu.SemaphoreType.DMA((8,)),
        ],
        compiler_params=params,
        cost_estimate=cost(10**9, 8 * 10**6),
    )(
        received, ab, tiles, cols,
        s_all, gg, lm, jnp.asarray(TILE_SPREAD, BF), qq, p0, idx, out_hot, factors.reshape(NI, COLE * NI),
    )
    got = hold(lax.all_to_all(payload, "elem", split_axis=0, concat_axis=0, tiled=True))
    local = pl.pallas_call(
        local_kernel,
        name="local",
        out_shape=shape((SLOTS, 256), F32),
        in_specs=[VMEM] * 2,
        out_specs=VMEM,
        compiler_params=params,
        cost_estimate=cost(3 * 10**8, 2 * 10**6),
    )(turned, contrib)
    partial = pl.pallas_call(
        place_kernel,
        name="place",
        out_shape=shape((4, FDEV, 256), BF),
        in_specs=[VMEM] * 2,
        out_specs=VMEM,
        compiler_params=params,
        cost_estimate=cost(10**8, 10**6),
    )(got, local)
    parts = hold(lax.all_to_all(partial, "section", split_axis=0, concat_axis=0, tiled=True))
    outs = pl.pallas_call(
        sum_kernel,
        name="total",
        out_shape=(shape((3, NF, FDEV), F32), shape((3, NF, FDEV), F32)),
        in_specs=[VMEM],
        out_specs=[VMEM] * 2,
        compiler_params=params,
        cost_estimate=cost(10**6, 10**6),
    )(parts)
    return tuple(out.transpose(0, 2, 1) for out in outs)


def solution(mesh):
    return jax.shard_map(
        on_device,
        mesh=mesh,
        in_specs=(
            P(None, "elem", "section", None, None),
            P(None, "elem", "section", None, None, None),
            P(None, "elem", "section", None, None, None),
            P("elem", None, None, None, None),
            P("elem", None, None, None),
            P("elem", None, None, None, None),
            P(),
            P(),
            P("section", "elem", None, None),
        ),
        out_specs=(P(None, ("section", "elem"), None), P(None, ("section", "elem"), None)),
        check_vma=False,
    )
```

```python
import jax
import jax.numpy as jnp
import numpy as np
from jax import lax
from jax.experimental import pallas as pl
from jax.experimental.pallas import tpu as pltpu
from jax.sharding import PartitionSpec as P

TI = (
    (4.325579890063155, 0.33919925181580984, 0.5417705399358749),
    (-4.178718591551905, -0.32768282076106237, 0.47662355450055044),
    (-0.5028726349457868, 2.571926949855605, -0.5960392048282249),
)
VARS, MODES, FN, NI, NF = 5, 20, 10, 100, 50
ELEMS, COLE, GRP, COLS, FDEV = 48, 192, 64, 128, 96
SLOTS = 4 * FDEV
W = 512
UW = VARS * W
CH = 3200
BF, F32, I32 = jnp.bfloat16, jnp.float32, jnp.int32
VMEM = pl.BlockSpec(memory_space=pltpu.VMEM)


def code_tables():
    cols = np.full((16, UW), -1, np.int32)
    for u in range(VARS):
        for k in range(4):
            for o in range(2):
                for n in range(FN):
                    for v in range(VARS):
                        lane = u * W + k * 128 + o * 64 + n * VARS + v
                        cols[0, lane] = (v * 5 + u) * 4 + k
                        cols[1, lane] = k * 5 + u
                        cols[2, lane] = o * FN + n
                        cols[3, lane] = n * 4 + k
                        cols[4, lane] = u * 2 + o
                        cols[5, lane] = v if o == 0 else -1
                        cols[7, lane] = o
                        cols[8, lane] = k * 64 + n * VARS + v if o == 0 else -1
    lanes = np.arange(UW) % 128
    cols[6] = np.where(cols[0] < 0, lanes, (lanes // 64) * 64 + (lanes % 64) % 5)
    rows = np.full((256, 128), -1, np.int32)
    for i in range(256):
        if i % 64 < NF:
            rows[i, 0] = (i // 64) * 5 + i % 64 % 5
            rows[i, 1] = i % 64 // 5
    for x in range(2):
        for i in range(NI):
            rows[x * 128 + i, 2] = (i % 5) * 2 + x
            rows[x * 128 + i, 3] = i // 5
            rows[x * 128 + i, 4] = i % 5
    lane = np.arange(CH)
    spread = (np.arange(128)[:, None] == lane[None, :] % NI).astype(np.float32)
    return cols, rows, spread


COL_CODES, ROW_CODES, TILE_SPREAD = code_tables()


def dot(a, b):
    return lax.dot_general(a, b, (((1,), (0,)), ((), ())), preferred_element_type=F32)


def dot_t(a, b):
    return lax.dot_general(a, b, (((1,), (1,)), ((), ())), preferred_element_type=F32)


def iota(shape, dim):
    return lax.broadcasted_iota(I32, shape, dim)


def onehot(cond):
    return jnp.where(cond, 1.0, 0.0).astype(BF)


def split(x):
    hi = x.astype(BF)
    return hi, (x - hi.astype(F32)).astype(BF)


def pack_kernel(inner_ref, face_ref, trace_ref, out_ref, mix_ref):
    out_ref[...] = jnp.zeros(out_ref.shape, BF)
    mix_ref[...] = jnp.zeros(mix_ref.shape, BF)

    def place(g, lane, piece):
        cut = slice(lane, lane + piece.shape[1])
        if g == 0:
            out_ref[0, :, cut] = piece
        else:
            mix_ref[g - 1, :, cut] = piece

    for ref, lane in ((inner_ref, 0), (face_ref, 128), (trace_ref, 384)):
        vals = [ref[t].astype(F32) for t in range(3)]
        for g in range(3):
            mixed = TI[g][0] * vals[0] + TI[g][1] * vals[1] + TI[g][2] * vals[2]
            if lane == 0:
                place(g, 0, mixed.astype(BF))
            else:
                for k in range(4):
                    place(g, lane + 64 * k, mixed[:, k, :].astype(BF))
    row = iota((ELEMS, ELEMS), 0)
    pick = onehot(iota((ELEMS, ELEMS), 1) == 3 * (row & 15) + (row >> 4))
    for g in range(2):
        moved = dot(pick, mix_ref[g]).astype(BF)
        for t in range(3):
            out_ref[1 + t, 16 * g : 16 * g + 16, :] = moved[16 * t : 16 * t + 16]


def prep_kernel(
    stab_ref, orient_ref, faces_ref, lift_ref, mass_ref, cols_ref, rows_ref,
    s_ref, gg_ref, qq_ref, lm_ref, p0_ref, idx_ref, ab_ref, turned_ref, out_hot_ref,
):
    section = lax.axis_index("section")
    column = lax.axis_index("elem")
    row = iota((COLE, ELEMS), 0)
    third = section - 1
    target = jnp.where(
        section == 0, row, jnp.where(row < GRP, 48 * (row >> 4) + 3 * (row & 15) + third, -1)
    )
    face = faces_ref[...]
    block = ((face >> 5) * 43691) >> 17
    owner = block & (COLS - 1)
    slot = (block >> 7) * FDEV + face - block * FDEV
    away = owner != column
    fields = [jnp.where(away, owner + 1, 0), jnp.where(away, 0, 1), slot >> 5, slot & 31]
    fields = [field.astype(F32) for field in fields]
    stab = jnp.zeros((COLE, 100), F32)
    orient = jnp.zeros((COLE, 40), F32)
    codes = jnp.zeros((COLE, 16), F32)
    turned = jnp.zeros((16, COLE), F32)
    for s in range(4):
        pick = onehot(target == iota((COLE, ELEMS), 1) + ELEMS * s)
        stab = stab + dot_t(pick, stab_ref[s].astype(F32).reshape(100, ELEMS).astype(BF))
        orient = orient + dot_t(pick, orient_ref[s].astype(F32).reshape(40, ELEMS).astype(BF))
        field = jnp.concatenate([f[s] for f in fields], axis=0).astype(BF)
        codes = codes + dot_t(pick, field)
        turned = turned + dot_t(field, pick)
    ab_ref[...] = codes
    turned_ref[...] = turned
    stab = stab.astype(BF)
    spread_kn = onehot(iota((40, UW), 0) == cols_ref[3:4, :])
    for u in range(VARS):
        cut = slice(u * W, (u + 1) * W)
        expand = onehot(iota((100, W), 0) == cols_ref[0:1, cut])
        s_ref[:, cut] = dot(stab, expand).astype(BF)
    nodes = dot(orient.astype(BF), spread_kn[:, :W])
    idx_ref[...] = (VARS * nodes).astype(I32) + cols_ref[6:7, :W]
    pick_j = onehot(rows_ref[:, 1:2] == iota((256, FN), 1))
    eye = jnp.where(iota((FN, FN), 0) == iota((FN, FN), 1), 1.0, 0.0)
    mass = jnp.concatenate([eye, mass_ref[...].astype(F32)], axis=0).astype(BF)
    mass = dot_t(pick_j, mass).astype(BF)
    pick_m = onehot(rows_ref[:, 3:4] == iota((256, MODES), 1))
    lift = jnp.concatenate([lift_ref[n].astype(F32) for n in range(FN)], axis=0).astype(BF)
    lift = dot_t(pick_m, lift).astype(BF)
    for u in range(VARS):
        cut = slice(u * W, (u + 1) * W)
        full = dot(mass, onehot(iota((2 * FN, W), 0) == cols_ref[2:3, cut]))
        gg_ref[:, cut] = jnp.where(rows_ref[:, 0:1] == cols_ref[1:2, cut], full, 0.0).astype(BF)
        full = dot(lift, spread_kn[:, cut])
        qq_ref[:, cut] = jnp.where(rows_ref[:, 2:3] == cols_ref[4:5, cut], full, 0.0).astype(BF)
        if u == 0:
            keep = rows_ref[:128, 4:5] == cols_ref[5:6, cut]
            keep = keep & (cols_ref[5:6, cut] >= 0)
            lm_ref[...] = jnp.where(keep, full[:128], 0.0).astype(BF)
    p0_ref[...] = onehot(iota((256, W), 0) == cols_ref[8:9, :W])
    before = onehot(iota((COLE, COLE), 0) < iota((COLE, COLE), 1))
    count = jnp.zeros((COLS, 1), F32)
    own_iota = iota((COLS, COLE), 0) + 1
    for k in range(4):
        own = turned[k : k + 1, :].astype(I32)
        hot = own_iota == own
        hot_f = jnp.where(hot, 1.0, 0.0)
        rank = dot(hot_f.astype(BF), before) + count
        count = count + jnp.sum(hot_f, axis=1, keepdims=True)
        rank = jnp.sum(jnp.where(hot, rank, 0.0), axis=0, keepdims=True).astype(I32)
        key = jnp.where(own > 0, 2 * (own - 1) + rank, -1)
        out_hot_ref[k] = onehot(iota((2 * COLS, COLE), 0) == key)


def main_kernel(
    rec_ref, s_hbm, gg_hbm, lm_hbm, tile_hbm, qq_hbm, p0_hbm, idx_hbm, hot_hbm, ab_hbm, factor_ref,
    pay_ref, con_ref,
    s_ref, gg_ref, lm_ref, tile_ref, qq_ref, p0_ref, idx_ref, hot_ref, ab_ref, fac_ref,
    sol_ref, bd_ref, sem_ref, load_ref,
):
    section = lax.axis_index("section")
    pairs = (
        (gg_hbm, gg_ref), (s_hbm, s_ref), (lm_hbm, lm_ref), (tile_hbm, tile_ref),
        (qq_hbm, qq_ref.at[0:256]),
        (p0_hbm, p0_ref), (idx_hbm, idx_ref), (hot_hbm, hot_ref), (ab_hbm, ab_ref),
        (qq_hbm, qq_ref.at[256:512]),
    )

    def load(i):
        return pltpu.make_async_copy(pairs[i][0], pairs[i][1], load_ref.at[i])

    for i in range(4):
        load(i).start()

    def spread(sides, chunks):
        part = 8 * len(sides)
        for e in range(4):
            low, high = 800 * e // 128 * 128, -(-800 * (e + 1) // 128) * 128
            at = [slice(32 * c + 8 * e, 32 * c + 8 * e + 8) for c in range(chunks)]
            x = jnp.concatenate([side[cut] for cut in at for side in sides], axis=0).astype(BF)
            size = (x.shape[0], high - low)
            keep = (iota(size, 0) & 7) + 8 * e == ((iota(size, 1) + low) * 5243) >> 19
            x = jnp.where(keep, dot(x, tile_ref[:, low:high]), 0.0).astype(BF)
            for c in range(chunks):
                row = 4 * part * c + part * e
                bd_ref[row : row + part, low:high] = x[part * c : part * c + part]

    def fetch(c):
        cut = pl.ds(c * CH, CH)
        return pltpu.make_async_copy(factor_ref.at[:, cut], fac_ref.at[:, cut], sem_ref.at[c])

    def finish(x_in, number, parts, solve):
        total = number * parts

        def s_of(u):
            s = s_ref[:number, u * W : (u + 1) * W].astype(F32)
            return jnp.concatenate([s] * parts, axis=0) if parts > 1 else s

        trace = x_in[:, 384:640]
        bd_ref[: 2 * total, :] = jnp.zeros((2 * total, CH), BF)
        sol_ref[...] = jnp.zeros(sol_ref.shape, F32)
        value = jnp.zeros((total, W), F32)
        load(0).wait()
        load(1).wait()
        for u in range(VARS):
            value = value + s_of(u) * dot(trace, gg_ref[:, u * W : (u + 1) * W])
        hi, lo = split(value)
        load(2).wait()
        lifted = (dot_t(hi, lm_ref[...]) + dot_t(lo, lm_ref[...])).astype(BF)
        lifted = lifted.astype(F32)
        load(3).wait()
        solve(x_in[:, :128].astype(F32), lifted)
        both = jnp.concatenate(split(sol_ref[:total, :]), axis=1)
        for i in range(4, 10):
            load(i).wait()
        base = jnp.where((iota((total, W), 1) & 64) != 0, value, 0.0) + dot(x_in[:, 128:384], p0_ref[...])
        for u in range(VARS):
            cut = slice(u * W, (u + 1) * W)
            base = base - s_of(u) * dot(both, qq_ref[:, cut])
        con_ref[...] = jnp.zeros(con_ref.shape, BF)
        lane = iota((number, 128), 1)
        pay = [jnp.zeros((2 * COLS, 128), F32) for _ in range(parts)]
        for k in range(4):
            index = idx_ref[:number, 128 * k : 128 * k + 128]
            for c in range(parts):
                piece = base[c * number : (c + 1) * number, 128 * k : 128 * k + 128]
                piece = jnp.take_along_axis(piece, index, axis=1, mode="promise_in_bounds")
                if c == 0:
                    piece = jnp.where(lane == NF, ab_ref[:number, 8 + k : 9 + k], piece)
                    piece = jnp.where(lane == NF + 1, ab_ref[:number, 12 + k : 13 + k], piece)
                piece = piece.astype(BF)
                con_ref[k, :number, 128 * c : 128 * c + 128] = piece
                pay[c] = pay[c] + dot(hot_ref[k, :, :number], piece)
        if parts == 1:
            pay = pay + [jnp.zeros((2 * COLS, 128), F32)]
        pay = jnp.concatenate(pay, axis=1)
        pay_ref[...] = pay.reshape(COLS, 2, 256).astype(BF)

    @pl.when(section == 0)
    def _():
        for c in range(6):
            fetch(c).start()
        for i in range(4, 10):
            load(i).start()
        x_in = jnp.concatenate([rec_ref[s] for s in range(4)], axis=0)

        def solve(inner, lifted):
            spread([inner, lifted], 6)
            for c in range(6):
                fetch(c).wait()
                y = dot_t(bd_ref[64 * c : 64 * c + 64, :], fac_ref[:, c * CH : (c + 1) * CH])
                for e in range(4):
                    cut = slice(32 * c + 8 * e, 32 * c + 8 * e + 8)
                    sol_ref[cut, 0:NI] = y[16 * e : 16 * e + 8]
                    sol_ref[cut, 128 : 128 + NI] = y[16 * e + 8 : 16 * e + 16]

        finish(x_in, COLE, 1, solve)

    @pl.when(section != 0)
    def _():
        for c in range(4):
            fetch(c).start()
        for i in range(4, 10):
            load(i).start()
        x_in = jnp.concatenate(
            [rec_ref[s, 16 * g : 16 * g + 16] for g in range(2) for s in range(4)], axis=0
        )

        def solve(inner, lifted):
            spread([inner[:GRP], lifted[:GRP], inner[GRP:], lifted[GRP:]], 2)
            for c in range(2):
                x = bd_ref[128 * c : 128 * c + 128, :]
                fetch(c).wait()
                a = dot_t(x, fac_ref[:, c * CH : (c + 1) * CH])
                fetch(2 + c).wait()
                b = dot_t(x, fac_ref[:, (2 + c) * CH : (3 + c) * CH])
                for e in range(4):
                    re, im = slice(32 * e, 32 * e + 16), slice(32 * e + 16, 32 * e + 32)
                    both = (a[re] - b[im], b[re] + a[im])
                    for g in range(2):
                        row = GRP * g + 32 * c + 8 * e
                        sol_ref[row : row + 8, 0:NI] = both[g][:8]
                        sol_ref[row : row + 8, 128 : 128 + NI] = both[g][8:]

        finish(x_in, GRP, 2, solve)


def local_kernel(turned_ref, con_ref, out_ref):
    total = jnp.zeros(out_ref.shape, F32)
    for k in range(4):
        slots = 32.0 * turned_ref[8 + k : 9 + k, :] + turned_ref[12 + k : 13 + k, :]
        slots = jnp.where(turned_ref[4 + k : 5 + k, :] > 0.5, slots, -1.0).astype(I32)
        total = total + dot(onehot(iota((SLOTS, COLE), 0) == slots), con_ref[k])
    out_ref[...] = total


def place_kernel(got_ref, loc_hbm, out_ref, loc_ref, sem_ref):
    load = pltpu.make_async_copy(loc_hbm, loc_ref, sem_ref)
    load.start()
    got = got_ref[...].astype(F32).reshape(2 * COLS, 256).astype(BF)
    lane = iota((8, 128), 1)
    weights = jnp.where(lane == NF, 32.0, jnp.where(lane == NF + 1, 1.0, 0.0)).astype(BF)
    slot = dot_t(weights, got[:, :128])[0:1].astype(I32)
    hot = onehot(iota((SLOTS, 2 * COLS), 0) == slot)
    total = dot(hot, got)
    load.wait()
    total = total + loc_ref[...]
    for s in range(4):
        out_ref[s] = total[FDEV * s : FDEV * s + FDEV].astype(BF)


def sum_kernel(got_ref, res_ref, schur_ref):
    three = got_ref[1].astype(F32) + got_ref[2].astype(F32) + got_ref[3].astype(F32)
    for g, part in enumerate((got_ref[0, :, :128].astype(F32), three[:, :128], three[:, 128:])):
        part = part.T
        res_ref[g] = part[:NF]
        schur_ref[g] = part[64 : 64 + NF]


def shape(dims, kind):
    return jax.ShapeDtypeStruct(dims, kind)


def on_chip(dims, kind):
    return pltpu.VMEM(dims, kind)


def hold(x):
    return pltpu.with_memory_space_constraint(x, pltpu.VMEM)


def cost(flops, nbytes):
    return pl.CostEstimate(flops=flops, bytes_accessed=nbytes, transcendentals=0)


def on_device(
    interior_res, face_res, trace_vals, stabil, element_faces, orient, lift_matrix, face_matrix, factors
):
    params = pltpu.CompilerParams(vmem_limit_bytes=59 * 2**20)
    send = pl.pallas_call(
        pack_kernel,
        name="pack",
        out_shape=shape((4, ELEMS, 640), BF),
        in_specs=[VMEM] * 3,
        out_specs=VMEM,
        scratch_shapes=[pltpu.VMEM((2, ELEMS, 640), BF)],
        compiler_params=params,
        cost_estimate=cost(10**8, 10**6),
    )(
        interior_res.reshape(3, ELEMS, NI),
        face_res.reshape(3, ELEMS, 4, NF),
        trace_vals.reshape(3, ELEMS, 4, NF),
    )
    received = hold(lax.all_to_all(send, "section", split_axis=0, concat_axis=0, tiled=True))
    cols, rows = jnp.asarray(COL_CODES), jnp.asarray(ROW_CODES)
    s_all, gg, qq, lm, p0, idx, ab, turned, out_hot = pl.pallas_call(
        prep_kernel,
        name="prep",
        out_shape=(
            shape((COLE, UW), BF),
            shape((256, UW), BF),
            shape((256, UW), BF),
            shape((128, W), BF),
            shape((256, W), BF),
            shape((COLE, W), I32),
            shape((COLE, 16), F32),
            shape((16, COLE), F32),
            shape((4, 2 * COLS, COLE), BF),
        ),
        in_specs=[VMEM] * 7,
        out_specs=[VMEM] * 9,
        compiler_params=params,
        cost_estimate=cost(10**9, 8 * 10**6),
    )(
        stabil[0].transpose(0, 3, 2, 1),
        orient[0].transpose(0, 3, 2, 1),
        element_faces[0].transpose(0, 2, 1),
        lift_matrix.transpose(2, 0, 1),
        face_matrix,
        cols,
        rows,
    )
    payload, contrib = pl.pallas_call(
        main_kernel,
        name="condense",
        out_shape=(shape((COLS, 2, 256), BF), shape((4, COLE, 256), BF)),
        in_specs=[VMEM] + [pl.BlockSpec(memory_space=pltpu.HBM)] * 10,
        out_specs=[VMEM] * 2,
        scratch_shapes=[
            pltpu.VMEM((COLE, UW), BF),
            pltpu.VMEM((256, UW), BF),
            pltpu.VMEM((128, W), BF),
            pltpu.VMEM((128, CH), BF),
            pltpu.VMEM((512, UW), BF),
            pltpu.VMEM((256, W), BF),
            pltpu.VMEM((COLE, W), I32),
            pltpu.VMEM((4, 2 * COLS, COLE), BF),
            pltpu.VMEM((COLE, 16), F32),
            pltpu.VMEM((NI, COLE * NI), BF),
            pltpu.VMEM((COLE, 256), F32),
            pltpu.VMEM((2 * COLE, CH), BF),
            pltpu.SemaphoreType.DMA((6,)),
            pltpu.SemaphoreType.DMA((10,)),
        ],
        compiler_params=params,
        cost_estimate=cost(10**9, 8 * 10**6),
    )(
        received, s_all, gg, lm, jnp.asarray(TILE_SPREAD, BF), qq, p0, idx, out_hot, ab, factors.reshape(NI, COLE * NI),
    )
    got = hold(lax.all_to_all(payload, "elem", split_axis=0, concat_axis=0, tiled=True))
    local = pl.pallas_call(
        local_kernel,
        name="local",
        out_shape=shape((SLOTS, 256), F32),
        in_specs=[VMEM] * 2,
        out_specs=VMEM,
        compiler_params=params,
        cost_estimate=cost(3 * 10**8, 2 * 10**6),
    )(turned, contrib)
    partial = pl.pallas_call(
        place_kernel,
        name="place",
        out_shape=on_chip((4, FDEV, 256), BF),
        in_specs=[VMEM, pl.BlockSpec(memory_space=pltpu.HBM)],
        out_specs=VMEM,
        scratch_shapes=[pltpu.VMEM((SLOTS, 256), F32), pltpu.SemaphoreType.DMA(())],
        compiler_params=params,
        cost_estimate=cost(10**8, 10**6),
    )(got, local)
    parts = hold(lax.all_to_all(partial, "section", split_axis=0, concat_axis=0, tiled=True))
    outs = pl.pallas_call(
        sum_kernel,
        name="total",
        out_shape=(shape((3, NF, FDEV), F32), shape((3, NF, FDEV), F32)),
        in_specs=[VMEM],
        out_specs=[VMEM] * 2,
        compiler_params=params,
        cost_estimate=cost(10**6, 10**6),
    )(parts)
    return tuple(out.transpose(0, 2, 1) for out in outs)


def solution(mesh):
    return jax.shard_map(
        on_device,
        mesh=mesh,
        in_specs=(
            P(None, "elem", "section", None, None),
            P(None, "elem", "section", None, None, None),
            P(None, "elem", "section", None, None, None),
            P("elem", None, None, None, None),
            P("elem", None, None, None),
            P("elem", None, None, None, None),
            P(),
            P(),
            P("section", "elem", None, None),
        ),
        out_specs=(P(None, ("section", "elem"), None), P(None, ("section", "elem"), None)),
        check_vma=False,
    )
```

```python
import jax
import jax.numpy as jnp
import numpy as np
from jax import lax
from jax.experimental import pallas as pl
from jax.experimental.pallas import tpu as pltpu
from jax.sharding import PartitionSpec as P

TI = (
    (4.325579890063155, 0.33919925181580984, 0.5417705399358749),
    (-4.178718591551905, -0.32768282076106237, 0.47662355450055044),
    (-0.5028726349457868, 2.571926949855605, -0.5960392048282249),
)
VARS, MODES, FN, NI, NF = 5, 20, 10, 100, 50
ELEMS, COLE, GRP, COLS, FDEV = 48, 192, 64, 128, 96
SLOTS = 4 * FDEV
W = 512
UW = VARS * W
CH = 3200
BF, F32, I32 = jnp.bfloat16, jnp.float32, jnp.int32
VMEM = pl.BlockSpec(memory_space=pltpu.VMEM)


def code_tables():
    cols = np.full((16, UW), -1, np.int32)
    for u in range(VARS):
        for k in range(4):
            for o in range(2):
                for n in range(FN):
                    for v in range(VARS):
                        lane = u * W + k * 128 + o * 64 + n * VARS + v
                        cols[0, lane] = (v * 5 + u) * 4 + k
                        cols[1, lane] = k * 5 + u
                        cols[2, lane] = o * FN + n
                        cols[3, lane] = n * 4 + k
                        cols[4, lane] = u * 2 + o
                        cols[5, lane] = v if o == 0 else -1
                        cols[7, lane] = o
                        cols[8, lane] = k * 64 + n * VARS + v if o == 0 else -1
    lanes = np.arange(UW) % 128
    cols[6] = np.where(cols[0] < 0, lanes, (lanes // 64) * 64 + (lanes % 64) % 5)
    rows = np.full((256, 128), -1, np.int32)
    for i in range(256):
        if i % 64 < NF:
            rows[i, 0] = (i // 64) * 5 + i % 64 % 5
            rows[i, 1] = i % 64 // 5
    for x in range(2):
        for i in range(NI):
            rows[x * 128 + i, 2] = (i % 5) * 2 + x
            rows[x * 128 + i, 3] = i // 5
            rows[x * 128 + i, 4] = i % 5
    lane = np.arange(CH)
    spread = (np.arange(128)[:, None] == lane[None, :] % NI).astype(np.float32)
    return cols, rows, spread


COL_CODES, ROW_CODES, TILE_SPREAD = code_tables()


def dot(a, b):
    return lax.dot_general(a, b, (((1,), (0,)), ((), ())), preferred_element_type=F32)


def dot_t(a, b):
    return lax.dot_general(a, b, (((1,), (1,)), ((), ())), preferred_element_type=F32)


def iota(shape, dim):
    return lax.broadcasted_iota(I32, shape, dim)


def onehot(cond):
    return jnp.where(cond, 1.0, 0.0).astype(BF)


def split(x):
    hi = x.astype(BF)
    return hi, (x - hi.astype(F32)).astype(BF)


def pack_kernel(inner_ref, face_ref, trace_ref, out_ref, mix_ref, row_ref):
    out_ref[...] = jnp.zeros(out_ref.shape, BF)
    mix_ref[...] = jnp.zeros(mix_ref.shape, BF)

    def place(g, lane, piece):
        cut = slice(lane, lane + piece.shape[1])
        if g == 0:
            out_ref[0, :, cut] = piece
        else:
            mix_ref[g - 1, :, cut] = piece

    for ref, lane in ((inner_ref, 0), (face_ref, 128), (trace_ref, 384)):
        vals = [ref[t].astype(F32) for t in range(3)]
        if lane > 0:
            vals = [val.reshape(COLE, NF) for val in vals]
        for g in range(3):
            mixed = TI[g][0] * vals[0] + TI[g][1] * vals[1] + TI[g][2] * vals[2]
            if lane == 0:
                place(g, 0, mixed.astype(BF))
            else:
                at = g if lane == 128 else 3 + g
                row_ref[at] = mixed
                for k in range(4):
                    piece = row_ref[at, pl.ds(k, ELEMS, stride=4), :]
                    place(g, lane + 64 * k, piece.astype(BF))
    row = iota((ELEMS, ELEMS), 0)
    pick = onehot(iota((ELEMS, ELEMS), 1) == 3 * (row & 15) + (row >> 4))
    for g in range(2):
        moved = dot(pick, mix_ref[g]).astype(BF)
        for t in range(3):
            out_ref[1 + t, 16 * g : 16 * g + 16, :] = moved[16 * t : 16 * t + 16]


def prep_kernel(
    stab_ref, orient_ref, faces_ref, lift_ref, mass_ref, cols_ref, rows_ref,
    s_ref, gg_ref, qq_ref, lm_ref, p0_ref, idx_ref, ab_ref, turned_ref, out_hot_ref,
):
    section = lax.axis_index("section")
    column = lax.axis_index("elem")
    row = iota((COLE, ELEMS), 0)
    third = section - 1
    target = jnp.where(
        section == 0, row, jnp.where(row < GRP, 48 * (row >> 4) + 3 * (row & 15) + third, -1)
    )
    face = faces_ref[...]
    block = ((face >> 5) * 43691) >> 17
    owner = block & (COLS - 1)
    slot = (block >> 7) * FDEV + face - block * FDEV
    away = owner != column
    fields = [jnp.where(away, owner + 1, 0), jnp.where(away, 0, 1), slot >> 5, slot & 31]
    fields = [field.astype(F32) for field in fields]
    stab = jnp.zeros((COLE, 100), F32)
    orient = jnp.zeros((COLE, 40), F32)
    codes = jnp.zeros((COLE, 16), F32)
    turned = jnp.zeros((16, COLE), F32)
    for s in range(4):
        pick = onehot(target == iota((COLE, ELEMS), 1) + ELEMS * s)
        stab = stab + dot_t(pick, stab_ref[s].astype(F32).reshape(100, ELEMS).astype(BF))
        orient = orient + dot_t(pick, orient_ref[s].astype(F32).reshape(40, ELEMS).astype(BF))
        field = jnp.concatenate([f[s] for f in fields], axis=0).astype(BF)
        codes = codes + dot_t(pick, field)
        turned = turned + dot_t(field, pick)
    ab_ref[...] = codes
    turned_ref[...] = turned
    stab = stab.astype(BF)
    spread_kn = onehot(iota((40, W), 0) == cols_ref[3:4, :W])
    for u in range(VARS):
        cut = slice(u * W, (u + 1) * W)
        expand = onehot(iota((100, W), 0) == cols_ref[0:1, cut])
        s_ref[:, cut] = dot(stab, expand).astype(BF)
    nodes = dot(orient.astype(BF), spread_kn)
    idx_ref[...] = (VARS * nodes).astype(I32) + cols_ref[6:7, :W]
    pick_j = onehot(rows_ref[:, 1:2] == iota((256, FN), 1))
    eye = jnp.where(iota((FN, FN), 0) == iota((FN, FN), 1), 1.0, 0.0)
    mass = jnp.concatenate([eye, mass_ref[...].astype(F32)], axis=0).astype(BF)
    mass = dot_t(pick_j, mass).astype(BF)
    pick_m = onehot(rows_ref[:, 3:4] == iota((256, MODES), 1))
    lift = jnp.concatenate([lift_ref[n].astype(F32) for n in range(FN)], axis=0).astype(BF)
    lift = dot_t(pick_m, lift).astype(BF)
    massed = dot(mass, onehot(iota((2 * FN, W), 0) == cols_ref[2:3, :W]))
    full = dot(lift, spread_kn)
    for u in range(VARS):
        cut = slice(u * W, (u + 1) * W)
        gg_ref[:, cut] = jnp.where(rows_ref[:, 0:1] == cols_ref[1:2, cut], massed, 0.0).astype(BF)
        qq_ref[:, cut] = jnp.where(rows_ref[:, 2:3] == cols_ref[4:5, cut], full, 0.0).astype(BF)
        if u == 0:
            keep = rows_ref[:128, 4:5] == cols_ref[5:6, cut]
            keep = keep & (cols_ref[5:6, cut] >= 0)
            lm_ref[...] = jnp.where(keep, full[:128], 0.0).astype(BF)
    p0_ref[...] = onehot(iota((256, W), 0) == cols_ref[8:9, :W])
    before = onehot(iota((COLE, COLE), 0) < iota((COLE, COLE), 1))
    count = jnp.zeros((COLS, 1), F32)
    own_iota = iota((COLS, COLE), 0) + 1
    for k in range(4):
        own = turned[k : k + 1, :].astype(I32)
        hot = own_iota == own
        hot_f = jnp.where(hot, 1.0, 0.0)
        rank = dot(hot_f.astype(BF), before) + count
        count = count + jnp.sum(hot_f, axis=1, keepdims=True)
        rank = jnp.sum(jnp.where(hot, rank, 0.0), axis=0, keepdims=True).astype(I32)
        key = jnp.where(own > 0, 2 * (own - 1) + rank, -1)
        out_hot_ref[k] = onehot(iota((2 * COLS, COLE), 0) == key)


def main_kernel(
    rec_ref, s_hbm, gg_hbm, lm_hbm, tile_hbm, qq_hbm, p0_hbm, idx_hbm, hot_hbm, ab_hbm, factor_ref,
    pay_ref, con_ref,
    s_ref, gg_ref, lm_ref, tile_ref, qq_ref, p0_ref, idx_ref, hot_ref, ab_ref, fac_ref,
    sol_ref, bd_ref, sem_ref, load_ref,
):
    section = lax.axis_index("section")
    pairs = (
        (gg_hbm, gg_ref), (s_hbm, s_ref), (lm_hbm, lm_ref), (tile_hbm, tile_ref),
        (qq_hbm, qq_ref.at[0:256]),
        (p0_hbm, p0_ref), (idx_hbm, idx_ref), (hot_hbm, hot_ref), (ab_hbm, ab_ref),
        (qq_hbm, qq_ref.at[256:512]),
    )

    def load(i):
        return pltpu.make_async_copy(pairs[i][0], pairs[i][1], load_ref.at[i])

    for i in range(4):
        load(i).start()

    def spread(sides, chunks):
        part = 8 * len(sides)
        for e in range(4):
            low, high = 800 * e // 128 * 128, -(-800 * (e + 1) // 128) * 128
            at = [slice(32 * c + 8 * e, 32 * c + 8 * e + 8) for c in range(chunks)]
            x = jnp.concatenate([side[cut] for cut in at for side in sides], axis=0).astype(BF)
            size = (x.shape[0], high - low)
            keep = (iota(size, 0) & 7) + 8 * e == ((iota(size, 1) + low) * 5243) >> 19
            x = jnp.where(keep, dot(x, tile_ref[:, low:high]), 0.0).astype(BF)
            for c in range(chunks):
                row = 4 * part * c + part * e
                bd_ref[row : row + part, low:high] = x[part * c : part * c + part]

    def fetch(c):
        cut = pl.ds(c * CH, CH)
        return pltpu.make_async_copy(factor_ref.at[:, cut], fac_ref.at[:, cut], sem_ref.at[c])

    def finish(x_in, number, parts, solve):
        total = number * parts

        def s_of(u):
            s = s_ref[:number, u * W : (u + 1) * W].astype(F32)
            return jnp.concatenate([s] * parts, axis=0) if parts > 1 else s

        trace = x_in[:, 384:640]
        bd_ref[: 2 * total, :] = jnp.zeros((2 * total, CH), BF)
        sol_ref[...] = jnp.zeros(sol_ref.shape, F32)
        value = jnp.zeros((total, W), F32)
        load(0).wait()
        load(1).wait()
        for u in range(VARS):
            value = value + s_of(u) * dot(trace, gg_ref[:, u * W : (u + 1) * W])
        hi, lo = split(value)
        load(2).wait()
        lifted = (dot_t(hi, lm_ref[...]) + dot_t(lo, lm_ref[...])).astype(BF)
        lifted = lifted.astype(F32)
        load(3).wait()
        solve(x_in[:, :128].astype(F32), lifted)
        both = jnp.concatenate(split(sol_ref[:total, :]), axis=1)
        for i in range(4, 10):
            load(i).wait()
        base = jnp.where((iota((total, W), 1) & 64) != 0, value, 0.0) + dot(x_in[:, 128:384], p0_ref[...])
        for u in range(VARS):
            cut = slice(u * W, (u + 1) * W)
            base = base - s_of(u) * dot(both, qq_ref[:, cut])
        con_ref[...] = jnp.zeros(con_ref.shape, BF)
        lane = iota((number, 128), 1)
        pay = [jnp.zeros((2 * COLS, 128), F32) for _ in range(parts)]
        for k in range(4):
            index = idx_ref[:number, 128 * k : 128 * k + 128]
            for c in range(parts):
                piece = base[c * number : (c + 1) * number, 128 * k : 128 * k + 128]
                piece = jnp.take_along_axis(piece, index, axis=1, mode="promise_in_bounds")
                if c == 0:
                    piece = jnp.where(lane == NF, ab_ref[:number, 8 + k : 9 + k], piece)
                    piece = jnp.where(lane == NF + 1, ab_ref[:number, 12 + k : 13 + k], piece)
                piece = piece.astype(BF)
                con_ref[k, :number, 128 * c : 128 * c + 128] = piece
                pay[c] = pay[c] + dot(hot_ref[k, :, :number], piece)
        if parts == 1:
            pay = pay + [jnp.zeros((2 * COLS, 128), F32)]
        pay = jnp.concatenate(pay, axis=1)
        pay_ref[...] = pay.reshape(COLS, 2, 256).astype(BF)

    @pl.when(section == 0)
    def _():
        for c in range(6):
            fetch(c).start()
        for i in range(4, 10):
            load(i).start()
        x_in = jnp.concatenate([rec_ref[s] for s in range(4)], axis=0)

        def solve(inner, lifted):
            spread([inner, lifted], 6)
            for c in range(6):
                fetch(c).wait()
                y = dot_t(bd_ref[64 * c : 64 * c + 64, :], fac_ref[:, c * CH : (c + 1) * CH])
                for e in range(4):
                    cut = slice(32 * c + 8 * e, 32 * c + 8 * e + 8)
                    sol_ref[cut, 0:NI] = y[16 * e : 16 * e + 8]
                    sol_ref[cut, 128 : 128 + NI] = y[16 * e + 8 : 16 * e + 16]

        finish(x_in, COLE, 1, solve)

    @pl.when(section != 0)
    def _():
        for c in range(4):
            fetch(c).start()
        for i in range(4, 10):
            load(i).start()
        x_in = jnp.concatenate(
            [rec_ref[s, 16 * g : 16 * g + 16] for g in range(2) for s in range(4)], axis=0
        )

        def solve(inner, lifted):
            spread([inner[:GRP], lifted[:GRP], inner[GRP:], lifted[GRP:]], 2)
            for c in range(2):
                x = bd_ref[128 * c : 128 * c + 128, :]
                fetch(c).wait()
                a = dot_t(x, fac_ref[:, c * CH : (c + 1) * CH])
                fetch(2 + c).wait()
                b = dot_t(x, fac_ref[:, (2 + c) * CH : (3 + c) * CH])
                for e in range(4):
                    re, im = slice(32 * e, 32 * e + 16), slice(32 * e + 16, 32 * e + 32)
                    both = (a[re] - b[im], b[re] + a[im])
                    for g in range(2):
                        row = GRP * g + 32 * c + 8 * e
                        sol_ref[row : row + 8, 0:NI] = both[g][:8]
                        sol_ref[row : row + 8, 128 : 128 + NI] = both[g][8:]

        finish(x_in, GRP, 2, solve)


def local_kernel(turned_ref, con_ref, out_ref):
    total = jnp.zeros(out_ref.shape, F32)
    for k in range(4):
        slots = 32.0 * turned_ref[8 + k : 9 + k, :] + turned_ref[12 + k : 13 + k, :]
        slots = jnp.where(turned_ref[4 + k : 5 + k, :] > 0.5, slots, -1.0).astype(I32)
        total = total + dot(onehot(iota((SLOTS, COLE), 0) == slots), con_ref[k])
    out_ref[...] = total


def place_kernel(got_ref, loc_hbm, out_ref, loc_ref, sem_ref):
    load = pltpu.make_async_copy(loc_hbm, loc_ref, sem_ref)
    load.start()
    got = got_ref[...].astype(F32).reshape(2 * COLS, 256).astype(BF)
    lane = iota((8, 128), 1)
    weights = jnp.where(lane == NF, 32.0, jnp.where(lane == NF + 1, 1.0, 0.0)).astype(BF)
    slot = dot_t(weights, got[:, :128])[0:1].astype(I32)
    hot = onehot(iota((SLOTS, 2 * COLS), 0) == slot)
    total = dot(hot, got)
    load.wait()
    total = total + loc_ref[...]
    for s in range(4):
        out_ref[s] = total[FDEV * s : FDEV * s + FDEV].astype(BF)


def sum_kernel(got_ref, res_ref, schur_ref):
    three = got_ref[1].astype(F32) + got_ref[2].astype(F32) + got_ref[3].astype(F32)
    for g, part in enumerate((got_ref[0, :, :128].astype(F32), three[:, :128], three[:, 128:])):
        part = part.T
        res_ref[g] = part[:NF]
        schur_ref[g] = part[64 : 64 + NF]


def shape(dims, kind):
    return jax.ShapeDtypeStruct(dims, kind)


def on_chip(dims, kind):
    return pltpu.VMEM(dims, kind)


def hold(x):
    return pltpu.with_memory_space_constraint(x, pltpu.VMEM)


def cost(flops, nbytes):
    return pl.CostEstimate(flops=flops, bytes_accessed=nbytes, transcendentals=0)


def on_device(
    interior_res, face_res, trace_vals, stabil, element_faces, orient, lift_matrix, face_matrix, factors
):
    params = pltpu.CompilerParams(vmem_limit_bytes=59 * 2**20)
    send = pl.pallas_call(
        pack_kernel,
        name="pack",
        out_shape=shape((4, ELEMS, 640), BF),
        in_specs=[VMEM] * 3,
        out_specs=VMEM,
        scratch_shapes=[pltpu.VMEM((2, ELEMS, 640), BF), pltpu.VMEM((6, COLE, NF), F32)],
        compiler_params=params,
        cost_estimate=cost(10**8, 10**6),
    )(
        interior_res.reshape(3, ELEMS, NI),
        face_res.reshape(3, ELEMS, 4, NF),
        trace_vals.reshape(3, ELEMS, 4, NF),
    )
    received = hold(lax.all_to_all(send, "section", split_axis=0, concat_axis=0, tiled=True))
    cols, rows = jnp.asarray(COL_CODES), jnp.asarray(ROW_CODES)
    s_all, gg, qq, lm, p0, idx, ab, turned, out_hot = pl.pallas_call(
        prep_kernel,
        name="prep",
        out_shape=(
            shape((COLE, UW), BF),
            shape((256, UW), BF),
            shape((256, UW), BF),
            shape((128, W), BF),
            shape((256, W), BF),
            shape((COLE, W), I32),
            shape((COLE, 16), F32),
            shape((16, COLE), F32),
            shape((4, 2 * COLS, COLE), BF),
        ),
        in_specs=[VMEM] * 7,
        out_specs=[VMEM] * 9,
        compiler_params=params,
        cost_estimate=cost(10**9, 8 * 10**6),
    )(
        stabil[0].transpose(0, 3, 2, 1),
        orient[0].transpose(0, 3, 2, 1),
        element_faces[0].transpose(0, 2, 1),
        lift_matrix.transpose(2, 0, 1),
        face_matrix,
        cols,
        rows,
    )
    payload, contrib = pl.pallas_call(
        main_kernel,
        name="condense",
        out_shape=(shape((COLS, 2, 256), BF), shape((4, COLE, 256), BF)),
        in_specs=[VMEM] + [pl.BlockSpec(memory_space=pltpu.HBM)] * 10,
        out_specs=[VMEM] * 2,
        scratch_shapes=[
            pltpu.VMEM((COLE, UW), BF),
            pltpu.VMEM((256, UW), BF),
            pltpu.VMEM((128, W), BF),
            pltpu.VMEM((128, CH), BF),
            pltpu.VMEM((512, UW), BF),
            pltpu.VMEM((256, W), BF),
            pltpu.VMEM((COLE, W), I32),
            pltpu.VMEM((4, 2 * COLS, COLE), BF),
            pltpu.VMEM((COLE, 16), F32),
            pltpu.VMEM((NI, COLE * NI), BF),
            pltpu.VMEM((COLE, 256), F32),
            pltpu.VMEM((2 * COLE, CH), BF),
            pltpu.SemaphoreType.DMA((6,)),
            pltpu.SemaphoreType.DMA((10,)),
        ],
        compiler_params=params,
        cost_estimate=cost(10**9, 8 * 10**6),
    )(
        received, s_all, gg, lm, jnp.asarray(TILE_SPREAD, BF), qq, p0, idx, out_hot, ab, factors.reshape(NI, COLE * NI),
    )
    got = hold(lax.all_to_all(payload, "elem", split_axis=0, concat_axis=0, tiled=True))
    local = pl.pallas_call(
        local_kernel,
        name="local",
        out_shape=shape((SLOTS, 256), F32),
        in_specs=[VMEM] * 2,
        out_specs=VMEM,
        compiler_params=params,
        cost_estimate=cost(3 * 10**8, 2 * 10**6),
    )(turned, contrib)
    partial = pl.pallas_call(
        place_kernel,
        name="place",
        out_shape=on_chip((4, FDEV, 256), BF),
        in_specs=[VMEM, pl.BlockSpec(memory_space=pltpu.HBM)],
        out_specs=VMEM,
        scratch_shapes=[pltpu.VMEM((SLOTS, 256), F32), pltpu.SemaphoreType.DMA(())],
        compiler_params=params,
        cost_estimate=cost(10**8, 10**6),
    )(got, local)
    parts = hold(lax.all_to_all(partial, "section", split_axis=0, concat_axis=0, tiled=True))
    outs = pl.pallas_call(
        sum_kernel,
        name="total",
        out_shape=(shape((3, NF, FDEV), F32), shape((3, NF, FDEV), F32)),
        in_specs=[VMEM],
        out_specs=[VMEM] * 2,
        compiler_params=params,
        cost_estimate=cost(10**6, 10**6),
    )(parts)
    return tuple(out.transpose(0, 2, 1) for out in outs)


def solution(mesh):
    return jax.shard_map(
        on_device,
        mesh=mesh,
        in_specs=(
            P(None, "elem", "section", None, None),
            P(None, "elem", "section", None, None, None),
            P(None, "elem", "section", None, None, None),
            P("elem", None, None, None, None),
            P("elem", None, None, None),
            P("elem", None, None, None, None),
            P(),
            P(),
            P("section", "elem", None, None),
        ),
        out_specs=(P(None, ("section", "elem"), None), P(None, ("section", "elem"), None)),
        check_vma=False,
    )
```
